32 devices in a mesh: depth: 2 (over core), seq: 16 (over z, y, x).
Axes of the slice: x: 2, y: 2, z: 4, core: 2. Of those that a mesh axis runs over, the one named last changes fastest.
Arguments:
- queries: bfloat16 [2, 2048, 4096], P('depth', 'seq'), may hold values from -27 to 27
- grad_out: bfloat16 [2, 2048, 4096], P('depth', 'seq'), may hold values from -48 to 48
- key_states: bfloat16 [2048, 4096], P('depth', 'seq'), may hold values from -3 to 3
- value_states: bfloat16 [2048, 4096], P('depth', 'seq'), may hold values from -6 to 6
- offsets: int32 [2], replicated, may hold values from 0 to 8, as said below
- windows: int32 [2], replicated, may hold values from 512 to 1024, as said below
Outputs:
- grad_queries: bfloat16 [2, 2048, 4096], P('depth', 'seq')
- grad_keys: bfloat16 [2048, 4096], P('depth', 'seq')
- grad_values: bfloat16 [2048, 4096], P('depth', 'seq')
The draws below stay inside these ranges and needn't reach their ends.
Inputs may be any that keep to these rules, and one draw needn't show every extreme that they name: `windows`: one depth's window is exactly 1024. `offsets`: one depth's offset is exactly 8.
All inputs are finite; a program needn't handle non-finite values.
Results may differ from the reference program's by a relative error of at most 0.033.
Values may be sent and summed in bfloat16 or wider, within the bound.
No kernel may reach another device: no remote copies, remote signals or barrier semaphores. Data moves between devices by JAX's collectives and lax.ppermute only.
A program may use at most 64 MiB of HBM per device.

```python
import math
import jax
import jax.numpy as jnp
from jax import lax

HEADS = 32
HEAD_DIM = 128
MODEL = 4096
DEPTHS = 2
SEQ_LEN = 2048
WIN = 1024
OFF_MAX = 8


def base_keys(key):
    table = jnp.clip(jax.random.normal(jax.random.fold_in(key, 41), (SEQ_LEN, MODEL), jnp.float32), -3.0, 3.0)
    return table


def draw_key_states(key, part):
    return base_keys(key).astype(jnp.bfloat16)


def draw_queries(key, part):
    table = jnp.clip(jax.random.normal(jax.random.fold_in(key, 51), (DEPTHS, SEQ_LEN, MODEL), jnp.float32), -4.0, 4.0)
    return table.astype(jnp.bfloat16)


def draw_offsets(key, part):
    drawn = jax.random.randint(jax.random.fold_in(key, 61), (DEPTHS,), 0, OFF_MAX + 1)
    chosen = jax.random.randint(jax.random.fold_in(key, 62), (), 0, DEPTHS)
    return drawn.at[chosen].set(OFF_MAX)


def draw_windows(key, part):
    drawn = jax.random.randint(jax.random.fold_in(key, 71), (DEPTHS,), WIN // 2, WIN + 1)
    chosen = jax.random.randint(jax.random.fold_in(key, 72), (), 0, DEPTHS)
    return drawn.at[chosen].set(WIN)


def block_scale(key, dims, shards, smallest, top_value):
    def one(position, shards_of):
        draws = jax.random.uniform(jax.random.fold_in(jax.random.fold_in(key, 6), position), (shards_of,), jnp.float32, smallest / len(shards), top_value / len(shards))
        return jnp.repeat(jnp.exp(draws), dims[position] // shards_of).reshape((-1,) + (1,) * (len(dims) - position - 1))

    gain = one(*shards[0])
    for cut in shards[1:]:
        gain = gain * one(*cut)
    return gain


def scatter_about(rng, dims, scale, limit, split=(), held_as=jnp.bfloat16):
    values = scale * jax.random.normal(rng, dims, jnp.float32)
    if split:
        values = values * block_scale(rng, dims, split, -0.22, 0.18)
    return jnp.clip(values, -limit, limit).astype(held_as)


def setup_inputs(seed: int = 0) -> dict:
    key_of = jax.random.split(jax.random.key(seed), 7)
    return {
        "queries": draw_queries(jax.random.fold_in(key_of[6], 71), 0),
        "grad_out": scatter_about(key_of[1], (DEPTHS, SEQ_LEN, MODEL), 8.0, 48.0, ((0, 2), (1, 16))),
        "key_states": draw_key_states(jax.random.fold_in(key_of[6], 71), 0),
        "value_states": scatter_about(key_of[3], (SEQ_LEN, MODEL), 1.0, 6.0, ((0, 2), (1, 16))),
        "offsets": draw_offsets(jax.random.fold_in(key_of[6], 71), 0),
        "windows": draw_windows(jax.random.fold_in(key_of[6], 71), 0),
    }


def allowed_mask(query_pos, key_pos, shift_now, span_now, seq_total):
    query_col = query_pos[:, None]
    key_row = key_pos[None, :]
    inside = (key_row >= 0) & (key_row < seq_total) & (query_col >= 0) & (query_col < seq_total)
    return inside & (key_row <= query_col + shift_now) & (key_row > query_col + shift_now - span_now)

def rounded(values_in):
    return lax.optimization_barrier(values_in.astype(jnp.bfloat16)).astype(jnp.float32)

def depth_terms(query3, grad3, key_pad, value_pad, shift_now, span_now, block_len):
    scaling = 1.0 / math.sqrt(HEAD_DIM)
    blocks = SEQ_LEN // block_len
    span_keys = block_len + WIN

    def backward(carry, number):
        key_acc, value_acc = carry
        first_row = number * block_len
        key_first = first_row + shift_now + 1
        query_blk = lax.dynamic_slice_in_dim(query3, first_row, block_len, 0).astype(jnp.float32)
        grad_blk = lax.dynamic_slice_in_dim(grad3, first_row, block_len, 0).astype(jnp.float32)
        key_blk = lax.dynamic_slice_in_dim(key_pad, key_first, span_keys, 0).astype(jnp.float32)
        value_blk = lax.dynamic_slice_in_dim(value_pad, key_first, span_keys, 0).astype(jnp.float32)
        scores = jnp.einsum('qhd,khd->hqk', query_blk, key_blk) * scaling
        query_pos = first_row + jnp.arange(block_len, dtype=jnp.int32)
        key_pos = key_first - WIN + jnp.arange(span_keys, dtype=jnp.int32)
        allowed = allowed_mask(query_pos, key_pos, shift_now, span_now, SEQ_LEN)
        masked = jnp.where(allowed[None], scores, -jnp.inf)
        highest = lax.optimization_barrier(jnp.max(masked, axis=2, keepdims=True))
        log_total = highest + jnp.log(lax.optimization_barrier(jnp.sum(jnp.exp(masked - highest), axis=2, keepdims=True)))
        probs = jnp.exp(masked - log_total)
        weights = rounded(probs)
        grad_probs = jnp.einsum('qhd,khd->hqk', grad_blk, value_blk)
        row_dot = lax.optimization_barrier(jnp.sum(weights * grad_probs, axis=2, keepdims=True))
        grad_scores = rounded(probs * (grad_probs - row_dot))
        grad_query = jnp.einsum('hqk,khd->qhd', grad_scores, key_blk) * scaling
        key_term = jnp.einsum('hqk,qhd->khd', grad_scores, query_blk) * scaling
        value_term = jnp.einsum('hqk,qhd->khd', weights, grad_blk)
        root = jnp.zeros((), jnp.int32)
        place = (key_first.astype(jnp.int32), root, root)
        key_acc = lax.dynamic_update_slice(key_acc, lax.dynamic_slice(key_acc, place, key_term.shape) + key_term, place)
        value_acc = lax.dynamic_update_slice(value_acc, lax.dynamic_slice(value_acc, place, value_term.shape) + value_term, place)
        return ((key_acc, value_acc), grad_query)
    padded_len = SEQ_LEN + WIN + OFF_MAX + 1
    start_acc = jnp.zeros((padded_len, HEADS, HEAD_DIM), jnp.float32)
    (key_acc, value_acc), grad_rows = lax.scan(backward, (start_acc, start_acc), jnp.arange(blocks, dtype=jnp.int32))
    grad_query = grad_rows.reshape(SEQ_LEN, MODEL)
    key_part = key_acc[WIN:WIN + SEQ_LEN].reshape(SEQ_LEN, MODEL)
    value_part = value_acc[WIN:WIN + SEQ_LEN].reshape(SEQ_LEN, MODEL)
    return (grad_query, key_part, value_part)

def reference(queries, grad_out, key_states, value_states, offsets, windows):
    block_len = min(512, SEQ_LEN // DEPTHS)
    widths = ((WIN, OFF_MAX + 1), (0, 0), (0, 0))
    key_pad = jnp.pad(key_states.reshape(SEQ_LEN, HEADS, HEAD_DIM), widths)
    value_pad = jnp.pad(value_states.reshape(SEQ_LEN, HEADS, HEAD_DIM), widths)
    grad_list = []
    key_sum = jnp.zeros((SEQ_LEN, MODEL), jnp.float32)
    value_sum = jnp.zeros((SEQ_LEN, MODEL), jnp.float32)
    for depth_id in range(DEPTHS):
        query3 = queries[depth_id].reshape(SEQ_LEN, HEADS, HEAD_DIM)
        grad3 = grad_out[depth_id].reshape(SEQ_LEN, HEADS, HEAD_DIM)
        grad_query, key_part, value_part = depth_terms(query3, grad3, key_pad, value_pad, offsets[depth_id], windows[depth_id], block_len)
        grad_list.append(grad_query.astype(jnp.bfloat16))
        key_sum = key_sum + rounded(key_part)
        value_sum = value_sum + rounded(value_part)
    return (jnp.stack(grad_list), key_sum.astype(jnp.bfloat16), value_sum.astype(jnp.bfloat16))
```

```python
import functools
import math

import jax
import jax.numpy as jnp
from jax import lax
from jax.experimental import pallas as pl
from jax.experimental.pallas import tpu as pltpu
from jax.sharding import PartitionSpec as P

HEAD_DIM = 128
WIN = 1024
WIN_MIN = 512
OFF_MAX = 8
EDGE = 16
SCALING = 1.0 / math.sqrt(HEAD_DIM)
EXP2_SCALE = SCALING * math.log2(math.e)


def nt_dot(a, b):
    return lax.dot_general(a, b, (((1,), (1,)), ((), ())), preferred_element_type=jnp.float32)


def nn_dot(a, b):
    return lax.dot_general(a, b, (((1,), (0,)), ((), ())), preferred_element_type=jnp.float32)


def backward_kernel(
    block, past, n_blocks,
    spans_ref, q_ref, g_ref, k_ref, v_ref,
    dq_ref, dk_ref, dv_ref,
    kt_ref, s_ref, p_ref, dk_acc, dv_acc,
):
    number = pl.program_id(1)
    shift = spans_ref[0]
    span = spans_ref[1]
    seq_total = n_blocks * block

    @pl.when(number == 0)
    def _():
        kt_ref[...] = k_ref[...].T
        dk_acc[...] = jnp.zeros_like(dk_acc)
        dv_acc[...] = jnp.zeros_like(dv_acc)

    def step(n_past):
        first_row = pl.multiple_of(number * block, block)
        query = q_ref[...]
        grad = g_ref[...]
        tiles = [
            (pl.multiple_of((number - back) * block, block), block, (n_past - back) * block, -back * block)
            for back in range(n_past, -1, -1)
        ]
        edge_first = pl.multiple_of(
            jnp.minimum(first_row + block, seq_total - EDGE), EDGE
        )
        edge_row = (n_past + 1) * block
        highest = jnp.full((1, block), -jnp.inf, jnp.float32)
        steps_off = lax.broadcasted_iota(jnp.int32, (block, block), 0) - lax.broadcasted_iota(
            jnp.int32, (block, block), 1
        )
        for key_first, rows, at, lead in tiles:
            score = nt_dot(k_ref[pl.ds(key_first, rows), :], query)
            if lead + block - 1 > 0:
                score = jnp.where(steps_off <= shift - lead, score, -jnp.inf)
            if lead - block + 1 <= OFF_MAX - WIN_MIN:
                score = jnp.where(steps_off > shift - span - lead, score, -jnp.inf)
            s_ref[pl.ds(at, rows), :] = score
            highest = jnp.maximum(highest, jnp.max(score, axis=0, keepdims=True))
        edge_score = nt_dot(k_ref[pl.ds(edge_first, EDGE), :], query)
        edge_key = edge_first + lax.broadcasted_iota(jnp.int32, (EDGE, block), 0)
        edge_query = first_row + lax.broadcasted_iota(jnp.int32, (EDGE, block), 1)
        edge_in = (edge_key >= first_row + block) & (edge_key - edge_query <= shift)
        edge_score = jnp.where(edge_in, edge_score, -jnp.inf)
        s_ref[pl.ds(edge_row, EDGE), :] = edge_score
        highest = jnp.maximum(highest, jnp.max(edge_score, axis=0, keepdims=True))

        tiles.append((edge_first, EDGE, edge_row, None))
        total = jnp.zeros((1, block), jnp.float32)
        dotted = jnp.zeros((1, block), jnp.float32)
        for key_first, rows, at, _ in tiles:
            part = jnp.exp2((s_ref[pl.ds(at, rows), :] - highest) * EXP2_SCALE)
            grad_prob = nt_dot(v_ref[pl.ds(key_first, rows), :], grad)
            s_ref[pl.ds(at, rows), :] = part
            p_ref[pl.ds(at, rows), :] = grad_prob
            total = total + jnp.sum(part, axis=0, keepdims=True)
            dotted = dotted + jnp.sum(part * grad_prob, axis=0, keepdims=True)
        inverse = 1.0 / total
        row_dot = dotted * inverse

        dq_t = jnp.zeros((HEAD_DIM, block), jnp.float32)
        for key_first, rows, at, _ in tiles:
            prob = s_ref[pl.ds(at, rows), :] * inverse
            weight = prob.astype(jnp.bfloat16)
            grad_score = (prob * (p_ref[pl.ds(at, rows), :] - row_dot)).astype(jnp.bfloat16)
            here = pl.ds(key_first, rows)
            dv_acc[here, :] += nn_dot(weight, grad)
            dk_acc[here, :] += nn_dot(grad_score, query)
            if rows == EDGE:
                dq_t = dq_t + lax.dot_general(
                    k_ref[here, :], grad_score, (((0,), (0,)), ((), ())),
                    preferred_element_type=jnp.float32,
                )
            else:
                dq_t = dq_t + nn_dot(kt_ref[:, here], grad_score)
        dq_ref[...] = (dq_t * SCALING).T.astype(jnp.bfloat16)

    for n_past in range(past):
        pl.when(number == n_past)(functools.partial(step, n_past))
    pl.when(number >= past)(functools.partial(step, past))

    @pl.when(number == n_blocks - 1)
    def _():
        dk_ref[...] = (dk_acc[...] * SCALING).astype(jnp.bfloat16)
        dv_ref[...] = dv_acc[...].astype(jnp.bfloat16)


def attention_backward(spans, query, grad, key, value):
    seq_total, width = query.shape
    heads = width // HEAD_DIM
    block = min(256, seq_total)
    n_blocks = seq_total // block
    past = min(WIN // block, n_blocks - 1)
    rows = (past + 1) * block + EDGE
    row_spec = pl.BlockSpec((block, HEAD_DIM), lambda h, i, _: (i, h))
    head_spec = pl.BlockSpec((seq_total, HEAD_DIM), lambda h, i, _: (0, h))
    whole = jax.ShapeDtypeStruct((seq_total, width), jnp.bfloat16)
    pairs = heads * seq_total * rows
    return pl.pallas_call(
        functools.partial(backward_kernel, block, past, n_blocks),
        grid_spec=pltpu.PrefetchScalarGridSpec(
            num_scalar_prefetch=1,
            grid=(heads, n_blocks),
            in_specs=[row_spec, row_spec, head_spec, head_spec],
            out_specs=[row_spec, head_spec, head_spec],
            scratch_shapes=[
                pltpu.VMEM((HEAD_DIM, seq_total), jnp.bfloat16),
                pltpu.VMEM((rows, block), jnp.float32),
                pltpu.VMEM((rows, block), jnp.float32),
                pltpu.VMEM((seq_total, HEAD_DIM), jnp.float32),
                pltpu.VMEM((seq_total, HEAD_DIM), jnp.float32),
            ],
        ),
        out_shape=[whole, whole, whole],
        cost_estimate=pl.CostEstimate(
            flops=10 * pairs * HEAD_DIM, bytes_accessed=14 * seq_total * width, transcendentals=pairs
        ),
        name="attention_backward",
    )(spans, query, grad, key, value)


def on_device(queries, grad_out, key_states, value_states, offsets, windows):
    depth_id = lax.axis_index("depth")
    depths = lax.axis_size("depth")
    seq_parts = lax.axis_size("seq")
    spans = jnp.stack([offsets[depth_id], windows[depth_id]])
    tok_rows = queries.shape[1]
    model_width = queries.shape[2]
    width = model_width // seq_parts
    seq_total = tok_rows * seq_parts
    key_rows = key_states.shape[0]

    both = jnp.concatenate([queries, grad_out], axis=0)
    both = jnp.transpose(both.reshape(2, tok_rows, seq_parts, width), (2, 0, 1, 3))
    both = lax.all_to_all(both, "seq", split_axis=0, concat_axis=0, tiled=True)
    query = both[:, 0].reshape(seq_total, width)
    grad = both[:, 1].reshape(seq_total, width)

    if depths == 2:
        swap = [(0, 1), (1, 0)]
        first = depth_id == 0

        def gather(mine):
            other = lax.ppermute(mine, "depth", swap)
            return jnp.concatenate(
                [jnp.where(first, mine, other), jnp.where(first, other, mine)], axis=0
            )

        def scatter(part):
            mine = lax.dynamic_slice_in_dim(part, depth_id * key_rows, key_rows, 0)
            given = lax.dynamic_slice_in_dim(part, (1 - depth_id) * key_rows, key_rows, 0)
            other = lax.ppermute(given, "depth", swap)
            return (mine.astype(jnp.float32) + other.astype(jnp.float32)).astype(jnp.bfloat16)
    else:

        def gather(mine):
            return lax.all_gather(mine, "depth", axis=0, tiled=True)

        def scatter(part):
            return lax.psum_scatter(part, "depth", scatter_dimension=0, tiled=True)

    key_all = gather(key_states)
    value_all = gather(value_states)
    dq, dk, dv = attention_backward(spans, query, grad, key_all, value_all)
    grad_keys = scatter(dk)
    grad_values = scatter(dv)
    back = lax.all_to_all(
        dq.reshape(seq_parts, tok_rows, width), "seq", split_axis=0, concat_axis=0, tiled=True
    )
    back = jnp.transpose(back, (1, 0, 2)).reshape(1, tok_rows, model_width)
    return back, grad_keys, grad_values


def solution(mesh):
    in_specs = (
        P("depth", "seq", None),
        P("depth", "seq", None),
        P("depth", "seq"),
        P("depth", "seq"),
        P(),
        P(),
    )
    out_specs = (P("depth", "seq", None), P("depth", "seq"), P("depth", "seq"))
    return jax.shard_map(
        on_device, mesh=mesh, in_specs=in_specs, out_specs=out_specs, check_vma=False
    )
```

```python
import functools
import math

import jax
import jax.numpy as jnp
from jax import lax
from jax.experimental import pallas as pl
from jax.experimental.pallas import tpu as pltpu
from jax.sharding import PartitionSpec as P


HEAD_DIM = 128
WIN = 1024
EDGE = 16
SCALING = 1.0 / math.sqrt(HEAD_DIM)
EXP2_SCALE = SCALING * math.log2(math.e)
LOWEST = -1e30


def nt_dot(a, b):
    return lax.dot_general(a, b, (((1,), (1,)), ((), ())), preferred_element_type=jnp.float32)


def nn_dot(a, b):
    return lax.dot_general(a, b, (((1,), (0,)), ((), ())), preferred_element_type=jnp.float32)


def backward_kernel(block, past, n_blocks, n_pieces, n_parts, *refs):
    scalars, *refs = refs
    if n_pieces == 1:
        q_ref, g_ref, *refs = refs
    else:
        pieces, refs = refs[:n_pieces], refs[n_pieces:]
    key_parts, refs = refs[:n_parts], refs[n_parts:]
    value_parts, refs = refs[:n_parts], refs[n_parts:]
    dq_ref, dk_ref, dv_ref, k_ref, v_ref, kt_ref, bias_ref, p_ref, gp_ref, dk_acc, dv_acc, *refs = refs

    number = pl.program_id(0)
    shift = scalars[0]
    span = scalars[1]
    seq_total = n_blocks * block

    @pl.when(number == 0)
    def _():
        part_rows = seq_total // n_parts
        for n in range(n_parts):
            here = pl.ds(pl.multiple_of(scalars[2 + n], part_rows), part_rows)
            k_ref[here, :] = key_parts[n][...]
            v_ref[here, :] = value_parts[n][...]
        kt_ref[...] = k_ref[...].T
        dk_acc[...] = jnp.zeros_like(dk_acc)
        dv_acc[...] = jnp.zeros_like(dv_acc)
        ahead = lax.broadcasted_iota(jnp.int32, (block, block), 0) - lax.broadcasted_iota(
            jnp.int32, (block, block), 1
        )
        for back in range(past + 1):
            here = ahead - back * block
            bias_ref[back] = jnp.where((here <= shift) & (here > shift - span), 0.0, -jnp.inf)
        if n_pieces > 1:
            places = pieces[0].shape[0]
            for n in range(n_pieces):
                refs[0][pl.ds(scalars[2 + n_parts + n], places)] = pieces[n][...]

    def step(n_past):
        first_row = pl.multiple_of(number * block, block)
        if n_pieces == 1:
            query = q_ref[...].reshape(block, HEAD_DIM)
            grad = g_ref[...].reshape(block, HEAD_DIM)
        else:
            rows = pieces[0].shape[2]
            held = refs[0][pl.ds(number * (block // rows), block // rows)]
            query = held[:, 0].reshape(block, HEAD_DIM)
            grad = held[:, 1].reshape(block, HEAD_DIM)
        edge_first = pl.multiple_of(jnp.minimum(first_row + block, seq_total - EDGE), EDGE)
        edge_key = edge_first + lax.broadcasted_iota(jnp.int32, (EDGE, block), 0)
        edge_query = first_row + lax.broadcasted_iota(jnp.int32, (EDGE, block), 1)
        edge_in = (edge_key >= first_row + block) & (edge_key - edge_query <= shift)
        tiles = [
            (pl.multiple_of((number - back) * block, block), block, back * block, back)
            for back in range(n_past + 1)
        ]
        tiles.append((edge_first, EDGE, (past + 1) * block, None))

        highest = jnp.full((1, block), LOWEST, jnp.float32)
        total = jnp.zeros((1, block), jnp.float32)
        dotted = jnp.zeros((1, block), jnp.float32)
        highs = []
        for key_first, rows, at, back in tiles:
            score = nt_dot(k_ref[pl.ds(key_first, rows), :], query)
            if back is None:
                score = jnp.where(edge_in, score, -jnp.inf)
            else:
                score = score + bias_ref[back]
            now = jnp.maximum(highest, jnp.max(score, axis=0, keepdims=True))
            part = jnp.exp2((score - now) * EXP2_SCALE)
            grad_prob = nt_dot(v_ref[pl.ds(key_first, rows), :], grad)
            p_ref[pl.ds(at, rows), :] = part
            gp_ref[pl.ds(at, rows), :] = grad_prob
            less = jnp.exp2((highest - now) * EXP2_SCALE)
            total = total * less + jnp.sum(part, axis=0, keepdims=True)
            dotted = dotted * less + jnp.sum(part * grad_prob, axis=0, keepdims=True)
            highest = now
            highs.append(now)
        inverse = 1.0 / total
        row_dot = dotted * inverse

        dq_t = jnp.zeros((HEAD_DIM, block), jnp.float32)
        for (key_first, rows, at, back), high in zip(tiles, highs, strict=True):
            prob = p_ref[pl.ds(at, rows), :] * (inverse * jnp.exp2((high - highest) * EXP2_SCALE))
            weight = prob.astype(jnp.bfloat16)
            grad_score = (prob * (gp_ref[pl.ds(at, rows), :] - row_dot)).astype(jnp.bfloat16)
            here = pl.ds(key_first, rows)
            dv_acc[here, :] += nn_dot(weight, grad)
            dk_acc[here, :] += nn_dot(grad_score, query)
            if back is None:
                dq_t = dq_t + lax.dot_general(
                    k_ref[here, :], grad_score, (((0,), (0,)), ((), ())),
                    preferred_element_type=jnp.float32,
                )
            else:
                dq_t = dq_t + nn_dot(kt_ref[:, here], grad_score)
        dq_ref[...] = (dq_t * SCALING).T.astype(jnp.bfloat16).reshape(dq_ref.shape)

    for n_past in range(past):
        pl.when(number == n_past)(functools.partial(step, n_past))
    pl.when(number >= past)(functools.partial(step, past))

    @pl.when(number == n_blocks - 1)
    def _():
        dk_ref[...] = (dk_acc[...] * SCALING).astype(jnp.bfloat16)
        dv_ref[...] = dv_acc[...].astype(jnp.bfloat16)


def attention_backward(scalars, pieces, key_parts, value_parts, head):
    n_pieces, n_parts = len(pieces), len(key_parts)
    places, _, tok_rows, _ = pieces[0].shape
    sources = places * n_pieces
    seq_total = sources * tok_rows
    block = min(2 * tok_rows, seq_total)
    per_block = block // tok_rows
    n_blocks = seq_total // block
    past = min(-(-WIN // block), n_blocks - 1)
    rows = (past + 1) * block + EDGE

    def whole(shape):
        return pl.BlockSpec(shape, lambda i, _: (0,) * len(shape))

    if n_pieces == 1:
        piece_args = [pieces[0], pieces[0]]
        piece_specs = [
            pl.BlockSpec((per_block, 1, tok_rows, HEAD_DIM), lambda i, _, w=which: (i, w, 0, 0))
            for which in range(2)
        ]
        piece_scratch = []
    else:
        piece_args = list(pieces)
        piece_specs = [whole(p.shape) for p in pieces]
        piece_scratch = [pltpu.VMEM((sources, 2, tok_rows, HEAD_DIM), jnp.bfloat16)]
    part_spec = pl.BlockSpec((seq_total // n_parts, HEAD_DIM), lambda i, _: (0, head))
    pairs = seq_total * rows
    f32, bf16 = jnp.float32, jnp.bfloat16
    return pl.pallas_call(
        functools.partial(backward_kernel, block, past, n_blocks, n_pieces, n_parts),
        grid_spec=pltpu.PrefetchScalarGridSpec(
            num_scalar_prefetch=1,
            grid=(n_blocks,),
            in_specs=piece_specs + [part_spec] * (2 * n_parts),
            out_specs=[
                pl.BlockSpec((per_block, tok_rows, HEAD_DIM), lambda i, _: (i, 0, 0)),
                whole((seq_total, HEAD_DIM)),
                whole((seq_total, HEAD_DIM)),
            ],
            scratch_shapes=[
                pltpu.VMEM((seq_total, HEAD_DIM), bf16),
                pltpu.VMEM((seq_total, HEAD_DIM), bf16),
                pltpu.VMEM((HEAD_DIM, seq_total), bf16),
                pltpu.VMEM((past + 1, block, block), f32),
                pltpu.VMEM((rows, block), f32),
                pltpu.VMEM((rows, block), f32),
                pltpu.VMEM((seq_total, HEAD_DIM), f32),
                pltpu.VMEM((seq_total, HEAD_DIM), f32),
            ]
            + piece_scratch,
        ),
        out_shape=[
            jax.ShapeDtypeStruct((sources, tok_rows, HEAD_DIM), bf16),
            jax.ShapeDtypeStruct((seq_total, HEAD_DIM), bf16),
            jax.ShapeDtypeStruct((seq_total, HEAD_DIM), bf16),
        ],
        cost_estimate=pl.CostEstimate(
            flops=10 * pairs * HEAD_DIM, bytes_accessed=14 * seq_total * HEAD_DIM, transcendentals=pairs
        ),
    )(scalars, *piece_args, *key_parts, *value_parts)


def moved(arrays, out_shapes, moves_of, scalars=None):
    n_in = len(arrays)

    def kernel(scalars_ref, *refs):
        ins, outs, sem = refs[:n_in], refs[n_in:-1], refs[-1]
        copies = [
            pltpu.make_async_copy(ins[a].at[source], outs[o].at[target], sem.at[n])
            for n, (a, source, o, target) in enumerate(moves_of(scalars_ref))
        ]
        for copy in copies:
            copy.start()
        for copy in copies:
            copy.wait()

    if scalars is None:
        scalars = jnp.zeros((1,), jnp.int32)
    count = len(moves_of(range(64)))
    return pl.pallas_call(
        kernel,
        in_specs=[pl.BlockSpec(memory_space=pltpu.SMEM)] + [pl.BlockSpec(memory_space=pl.ANY)] * n_in,
        out_specs=[pl.BlockSpec(memory_space=pltpu.VMEM)] * len(out_shapes),
        out_shape=[jax.ShapeDtypeStruct(s, jnp.bfloat16) for s in out_shapes],
        scratch_shapes=[pltpu.SemaphoreType.DMA((count,))],
        cost_estimate=pl.CostEstimate(
            flops=0, bytes_accessed=4 * sum(math.prod(s) for s in out_shapes), transcendentals=0
        ),
    )(scalars, *arrays)


def layout_of(parts):
    near = 1 << (parts.bit_length() // 2)
    far = parts // near
    return near, far, far * near == parts and parts & (parts - 1) == 0 and far > 1


def on_device(queries, grad_out, key_states, value_states, offsets, windows):
    depth_id = lax.axis_index("depth")
    seq_id = lax.axis_index("seq")
    depths = lax.axis_size("depth")
    parts = lax.axis_size("seq")
    tok_rows, model_width = queries.shape[1:]
    key_rows, width = key_states.shape
    heads = width // HEAD_DIM
    queries = queries.reshape(tok_rows, model_width)
    grad_out = grad_out.reshape(tok_rows, model_width)
    near, far, two_step = layout_of(parts)
    near_id, far_id = seq_id % near, seq_id // near
    piece = (2, tok_rows, HEAD_DIM)

    def column(dest, head):
        start = (dest * heads + head) * HEAD_DIM
        if not isinstance(start, int):
            start = pl.multiple_of(start, HEAD_DIM)
        return (slice(None), pl.ds(start, HEAD_DIM))

    def ppermute_xor(array, bits):
        return lax.ppermute(array, "seq", [(i, i ^ bits) for i in range(parts)])

    def send_all(head):
        (sent,) = moved(
            [queries, grad_out], [(parts, *piece)],
            lambda _: [(a, column(d, head), 0, (d, a)) for d in range(parts) for a in range(2)],
        )
        return [lax.all_to_all(sent, "seq", split_axis=0, concat_axis=0, tiled=True)]

    def send_near_then_far(head):
        ids = jnp.stack([near_id, far_id]).astype(jnp.int32)
        first = moved(
            [queries, grad_out], [(far, *piece)] * near,
            lambda s: [
                (a, column(f * near + (s[0] ^ j), head), j, (f, a))
                for j in range(near) for f in range(far) for a in range(2)
            ],
            ids,
        )
        first = [first[0]] + [ppermute_xor(first[j], j) for j in range(1, near)]
        second = moved(
            first, [(near, *piece)] * far,
            lambda s: [(j, s[1] ^ m, m, s[0] ^ j) for m in range(far) for j in range(near)],
            ids,
        )
        return [second[0]] + [ppermute_xor(second[m], m * near) for m in range(1, far)]

    received = [
        send_near_then_far(head) if head and two_step else send_all(head) for head in range(heads)
    ]

    if depths == 2:
        swap = [(0, 1), (1, 0)]
        key_parts = [key_states, lax.ppermute(key_states, "depth", swap)]
        value_parts = [value_states, lax.ppermute(value_states, "depth", swap)]
        starts = [depth_id * key_rows, (1 - depth_id) * key_rows]

        def summed(part):
            mine = lax.dynamic_slice_in_dim(part, depth_id * key_rows, key_rows, 0)
            given = lax.dynamic_slice_in_dim(part, (1 - depth_id) * key_rows, key_rows, 0)
            other = lax.ppermute(given, "depth", swap)
            return (mine.astype(jnp.float32) + other.astype(jnp.float32)).astype(jnp.bfloat16)
    else:
        key_parts = [lax.all_gather(key_states, "depth", axis=0, tiled=True)]
        value_parts = [lax.all_gather(value_states, "depth", axis=0, tiled=True)]
        starts = [0]

        def summed(part):
            return lax.psum_scatter(part, "depth", scatter_dimension=0, tiled=True)

    back, grad_keys, grad_values = [], [], []
    for head in range(heads):
        pieces = received[head]
        places = [0] if len(pieces) == 1 else [(far_id ^ m) * near for m in range(far)]
        scalars = jnp.stack(
            [jnp.asarray(v, jnp.int32) for v in (offsets[depth_id], windows[depth_id], *starts, *places)]
        )
        dq, dk, dv = attention_backward(scalars, pieces, key_parts, value_parts, head)
        back.append(lax.all_to_all(dq, "seq", split_axis=0, concat_axis=0, tiled=True))
        grad_keys.append(summed(dk))
        grad_values.append(summed(dv))

    (grad_queries,) = moved(
        back, [(tok_rows, model_width)],
        lambda _: [(h, d, 0, column(d, h)) for h in range(heads) for d in range(parts)],
    )
    return (
        grad_queries.reshape(1, tok_rows, model_width),
        jnp.concatenate(grad_keys, axis=1),
        jnp.concatenate(grad_values, axis=1),
    )


def solution(mesh):
    in_specs = (
        P("depth", "seq", None),
        P("depth", "seq", None),
        P("depth", "seq"),
        P("depth", "seq"),
        P(),
        P(),
    )
    out_specs = (P("depth", "seq", None), P("depth", "seq"), P("depth", "seq"))
    return jax.shard_map(
        on_device, mesh=mesh, in_specs=in_specs, out_specs=out_specs, check_vma=False
    )
```

```python
import functools
import math

import jax
import jax.numpy as jnp
from jax import lax
from jax.experimental import pallas as pl
from jax.experimental.pallas import tpu as pltpu
from jax.sharding import PartitionSpec as P


HEAD_DIM = 128
WIN = 1024
EDGE = 16
SCALING = 1.0 / math.sqrt(HEAD_DIM)
EXP2_SCALE = SCALING * math.log2(math.e)
LOWEST = -1e30


def nt_dot(a, b):
    return lax.dot_general(a, b, (((1,), (1,)), ((), ())), preferred_element_type=jnp.float32)


def nn_dot(a, b):
    return lax.dot_general(a, b, (((1,), (0,)), ((), ())), preferred_element_type=jnp.float32)


def backward_kernel(block, past, n_blocks, head, n_pieces, n_parts, *refs):
    offsets_ref, windows_ref, *refs = refs
    pieces, refs = refs[:n_pieces], refs[n_pieces:]
    key_parts, refs = refs[:n_parts], refs[n_parts:]
    value_parts, refs = refs[:n_parts], refs[n_parts:]
    dq_ref, *refs = refs
    sums, refs = refs[:n_parts], refs[n_parts:]
    held_ref, k_ref, v_ref, kt_ref, bias_ref, p_ref, gp_ref, dk_acc, dv_acc, sems = refs

    number = pl.program_id(0)
    depth_id, seq_id = lax.axis_index("depth"), lax.axis_index("seq")
    shift = offsets_ref[depth_id]
    span = windows_ref[depth_id]
    seq_total = n_blocks * block
    part_rows = seq_total // n_parts
    tok_rows = held_ref.shape[2]

    def part_at(n):
        return pl.ds(pl.multiple_of((depth_id ^ n) * part_rows, part_rows) if n_parts > 1 else 0, part_rows)

    @pl.when(number == 0)
    def _():
        columns = pl.ds(head * HEAD_DIM, HEAD_DIM)
        copies = []
        for n in range(n_parts):
            for parts, ref in ((key_parts, k_ref), (value_parts, v_ref)):
                copies.append((parts[n].at[:, columns], ref.at[part_at(n)]))
        for k in range(n_pieces):
            copies.append((pieces[k], held_ref.at[seq_id ^ k] if n_pieces > 1 else held_ref))
        copies = [
            pltpu.make_async_copy(source, target, sems.at[n])
            for n, (source, target) in enumerate(copies)
        ]
        for copy in copies:
            copy.start()
        dk_acc[...] = jnp.zeros_like(dk_acc)
        dv_acc[...] = jnp.zeros_like(dv_acc)
        ahead = lax.broadcasted_iota(jnp.int32, (8, block), 0) - lax.broadcasted_iota(
            jnp.int32, (8, block), 1
        )
        for back in range(past + 1):
            for row in range(0, block, 8):
                lead = row - back * block
                keep = ahead > shift - span - lead
                if lead + 7 > 0:
                    keep = keep & (ahead <= shift - lead)
                bias_ref[back, pl.ds(row, 8), :] = jnp.where(keep, 0.0, -jnp.inf)
        for copy in copies:
            copy.wait()
        kt_ref[...] = k_ref[...].T

    def step(n_past):
        first_row = pl.multiple_of(number * block, block)
        per_block = block // tok_rows
        held = pl.ds(number * per_block, per_block)
        query = held_ref[held, 0].reshape(block, HEAD_DIM)
        grad = held_ref[held, 1].reshape(block, HEAD_DIM)
        edge_first = pl.multiple_of(jnp.minimum(first_row + block, seq_total - EDGE), EDGE)
        edge_key = edge_first + lax.broadcasted_iota(jnp.int32, (EDGE, block), 0)
        edge_query = first_row + lax.broadcasted_iota(jnp.int32, (EDGE, block), 1)
        edge_in = (edge_key >= first_row + block) & (edge_key - edge_query <= shift)
        tiles = [
            (pl.multiple_of((number - back) * block, block), block, back * block, back)
            for back in range(n_past + 1)
        ]
        tiles.append((edge_first, EDGE, (past + 1) * block, None))

        highest = jnp.full((1, block), LOWEST, jnp.float32)
        total = jnp.zeros((1, block), jnp.float32)
        dotted = jnp.zeros((1, block), jnp.float32)
        highs = []
        for key_first, rows, at, back in tiles:
            score = nt_dot(k_ref[pl.ds(key_first, rows), :], query)
            if back is None:
                score = jnp.where(edge_in, score, -jnp.inf)
            else:
                score = score + bias_ref[back]
            now = jnp.maximum(highest, jnp.max(score, axis=0, keepdims=True))
            part = jnp.exp2((score - now) * EXP2_SCALE)
            grad_prob = nt_dot(v_ref[pl.ds(key_first, rows), :], grad)
            p_ref[pl.ds(at, rows), :] = part
            gp_ref[pl.ds(at, rows), :] = grad_prob
            less = jnp.exp2((highest - now) * EXP2_SCALE)
            total = total * less + jnp.sum(part, axis=0, keepdims=True)
            dotted = dotted * less + jnp.sum(part * grad_prob, axis=0, keepdims=True)
            highest = now
            highs.append(now)
        inverse = 1.0 / total
        row_dot = dotted * inverse

        dq_t = jnp.zeros((HEAD_DIM, block), jnp.float32)
        for (key_first, rows, at, back), high in zip(tiles, highs, strict=True):
            prob = p_ref[pl.ds(at, rows), :] * (inverse * jnp.exp2((high - highest) * EXP2_SCALE))
            weight = prob.astype(jnp.bfloat16)
            grad_score = (prob * (gp_ref[pl.ds(at, rows), :] - row_dot)).astype(jnp.bfloat16)
            here = pl.ds(key_first, rows)
            dv_acc[here, :] += nn_dot(weight, grad)
            dk_acc[here, :] += nn_dot(grad_score, query)
            if back is None:
                dq_t = dq_t + lax.dot_general(
                    k_ref[here, :], grad_score, (((0,), (0,)), ((), ())),
                    preferred_element_type=jnp.float32,
                )
            else:
                dq_t = dq_t + nn_dot(kt_ref[:, here], grad_score)
        dq_ref[...] = (dq_t * SCALING).T.astype(jnp.bfloat16).reshape(dq_ref.shape)

    for n_past in range(past):
        pl.when(number == n_past)(functools.partial(step, n_past))
    pl.when(number >= past)(functools.partial(step, past))

    @pl.when(number == n_blocks - 1)
    def _():
        for n in range(n_parts):
            sums[n][0] = (dk_acc[part_at(n), :] * SCALING).astype(jnp.bfloat16)
            sums[n][1] = dv_acc[part_at(n), :].astype(jnp.bfloat16)


def attention_backward(offsets, windows, pieces, key_parts, value_parts, head):
    n_pieces, n_parts = len(pieces), len(key_parts)
    tok_rows = pieces[0].shape[-2]
    seq_total = key_parts[0].shape[0] * n_parts
    sources = seq_total // tok_rows
    block = min(2 * tok_rows, seq_total)
    per_block = block // tok_rows
    n_blocks = seq_total // block
    past = min(-(-WIN // block), n_blocks - 1)
    rows = (past + 1) * block + EDGE
    pairs = seq_total * rows
    f32, bf16 = jnp.float32, jnp.bfloat16
    sums_shape = (2, seq_total // n_parts, HEAD_DIM)
    dq, *sums = pl.pallas_call(
        functools.partial(backward_kernel, block, past, n_blocks, head, n_pieces, n_parts),
        grid_spec=pltpu.PrefetchScalarGridSpec(
            num_scalar_prefetch=2,
            grid=(n_blocks,),
            in_specs=[pl.BlockSpec(memory_space=pl.ANY)] * (n_pieces + 2 * n_parts),
            out_specs=[pl.BlockSpec((per_block, tok_rows, HEAD_DIM), lambda i, *_: (i, 0, 0))]
            + [pl.BlockSpec(sums_shape, lambda i, *_: (0, 0, 0))] * n_parts,
            scratch_shapes=[
                pltpu.VMEM((sources, 2, tok_rows, HEAD_DIM), bf16),
                pltpu.VMEM((seq_total, HEAD_DIM), bf16),
                pltpu.VMEM((seq_total, HEAD_DIM), bf16),
                pltpu.VMEM((HEAD_DIM, seq_total), bf16),
                pltpu.VMEM((past + 1, block, block), f32),
                pltpu.VMEM((rows, block), f32),
                pltpu.VMEM((rows, block), f32),
                pltpu.VMEM((seq_total, HEAD_DIM), f32),
                pltpu.VMEM((seq_total, HEAD_DIM), f32),
                pltpu.SemaphoreType.DMA((n_pieces + 2 * n_parts,)),
            ],
        ),
        out_shape=[jax.ShapeDtypeStruct((sources, tok_rows, HEAD_DIM), bf16)]
        + [jax.ShapeDtypeStruct(sums_shape, bf16)] * n_parts,
        cost_estimate=pl.CostEstimate(
            flops=10 * pairs * HEAD_DIM, bytes_accessed=14 * seq_total * HEAD_DIM, transcendentals=pairs
        ),
    )(offsets, windows, *pieces, *key_parts, *value_parts)
    return dq, sums


def pack(head, heads, queries, grad_out, n_outs):
    tok_rows, model_width = queries.shape
    parts = model_width // (heads * HEAD_DIM)
    shape = (2, tok_rows, HEAD_DIM)

    def kernel(q_ref, g_ref, *refs):
        outs, (held, in_sems, out_sems) = refs[:n_outs], refs[n_outs:]
        seq_id = lax.axis_index("seq")
        loads, stores = [], []
        for k in range(parts):
            dest = seq_id ^ k if n_outs > 1 else k
            start = pl.multiple_of((dest * heads + head) * HEAD_DIM, HEAD_DIM)
            for a, ref in enumerate((q_ref, g_ref)):
                loads.append(
                    pltpu.make_async_copy(
                        ref.at[:, pl.ds(start, HEAD_DIM)], held.at[k, a], in_sems.at[k, a]
                    )
                )
            target = outs[k] if n_outs > 1 else outs[0].at[k]
            stores.append(pltpu.make_async_copy(held.at[k], target, out_sems.at[k]))
        for load in loads:
            load.start()
        for k in range(parts):
            loads[2 * k].wait()
            loads[2 * k + 1].wait()
            stores[k].start()
        for store in stores:
            store.wait()

    return pl.pallas_call(
        kernel,
        in_specs=[pl.BlockSpec(memory_space=pl.ANY)] * 2,
        out_specs=[pl.BlockSpec(memory_space=pl.ANY)] * n_outs,
        out_shape=[jax.ShapeDtypeStruct(shape if n_outs > 1 else (parts, *shape), jnp.bfloat16)] * n_outs,
        scratch_shapes=[
            pltpu.VMEM((parts, *shape), jnp.bfloat16),
            pltpu.SemaphoreType.DMA((parts, 2)),
            pltpu.SemaphoreType.DMA((parts,)),
        ],
        cost_estimate=pl.CostEstimate(
            flops=0, bytes_accessed=4 * parts * math.prod(shape), transcendentals=0
        ),
    )(queries, grad_out)


def unpack(back, tok_rows, model_width):
    heads = len(back)
    parts = back[0].shape[0]

    def kernel(*refs):
        ins, out, sems = refs[:heads], refs[heads], refs[heads + 1]
        copies = []
        for head in range(heads):
            for d in range(parts):
                columns = pl.ds((d * heads + head) * HEAD_DIM, HEAD_DIM)
                copies.append(
                    pltpu.make_async_copy(ins[head].at[d], out.at[:, columns], sems.at[head, d])
                )
        for copy in copies:
            copy.start()
        for copy in copies:
            copy.wait()

    return pl.pallas_call(
        kernel,
        in_specs=[pl.BlockSpec(memory_space=pl.ANY)] * heads,
        out_specs=pl.BlockSpec(memory_space=pltpu.VMEM),
        out_shape=jax.ShapeDtypeStruct((tok_rows, model_width), jnp.bfloat16),
        scratch_shapes=[pltpu.SemaphoreType.DMA((heads, parts))],
        compiler_params=pltpu.CompilerParams(vmem_limit_bytes=8 * 2**20),
        name="unpack",
    )(*back)


def on_device(queries, grad_out, key_states, value_states, offsets, windows):
    depths = lax.axis_size("depth")
    parts = lax.axis_size("seq")
    tok_rows, model_width = queries.shape[1:]
    heads = key_states.shape[1] // HEAD_DIM
    queries = queries.reshape(tok_rows, model_width)
    grad_out = grad_out.reshape(tok_rows, model_width)

    def received(head):
        if head + 1 < heads and parts & (parts - 1) == 0:
            sent = pack(head, heads, queries, grad_out, parts)
            landed = [sent[0]]
            for k in range(1, parts):
                landed.append(lax.ppermute(sent[k], "seq", [(i, i ^ k) for i in range(parts)]))
            return landed
        (sent,) = pack(head, heads, queries, grad_out, 1)
        return [lax.all_to_all(sent, "seq", split_axis=0, concat_axis=0, tiled=True)]

    pieces = [received(head) for head in range(heads)]

    swap = [(0, 1), (1, 0)]
    if depths == 2:
        key_parts = [key_states, lax.ppermute(key_states, "depth", swap)]
        value_parts = [value_states, lax.ppermute(value_states, "depth", swap)]
    else:
        key_parts = [lax.all_gather(key_states, "depth", axis=0, tiled=True)]
        value_parts = [lax.all_gather(value_states, "depth", axis=0, tiled=True)]

    def over_depths(sums):
        if depths == 2:
            other = lax.ppermute(sums[1], "depth", swap)
            return (sums[0].astype(jnp.float32) + other.astype(jnp.float32)).astype(jnp.bfloat16)
        return lax.psum_scatter(sums[0], "depth", scatter_dimension=1, tiled=True)

    back, totals = [], []
    for head in range(heads):
        dq, sums = attention_backward(offsets, windows, pieces[head], key_parts, value_parts, head)
        back.append(lax.all_to_all(dq, "seq", split_axis=0, concat_axis=0, tiled=True))
        totals.append(over_depths(sums))

    return (
        unpack(back, tok_rows, model_width).reshape(1, tok_rows, model_width),
        jnp.concatenate([total[0] for total in totals], axis=1),
        jnp.concatenate([total[1] for total in totals], axis=1),
    )


def solution(mesh):
    in_specs = (
        P("depth", "seq", None),
        P("depth", "seq", None),
        P("depth", "seq"),
        P("depth", "seq"),
        P(),
        P(),
    )
    out_specs = (P("depth", "seq", None), P("depth", "seq"), P("depth", "seq"))
    return jax.shard_map(
        on_device, mesh=mesh, in_specs=in_specs, out_specs=out_specs, check_vma=False
    )
```

```python
import functools
import math

import jax
import jax.numpy as jnp
from jax import lax
from jax.experimental import pallas as pl
from jax.experimental.pallas import tpu as pltpu
from jax.sharding import PartitionSpec as P


HEAD_DIM = 128
WIN = 1024
EDGE = 16
SCALING = 1.0 / math.sqrt(HEAD_DIM)
EXP2_SCALE = SCALING * math.log2(math.e)
LOWEST = -1e30


def nt_dot(a, b):
    return lax.dot_general(a, b, (((1,), (1,)), ((), ())), preferred_element_type=jnp.float32)


def nn_dot(a, b):
    return lax.dot_general(a, b, (((1,), (0,)), ((), ())), preferred_element_type=jnp.float32)


def aligned(value, size):
    return value if isinstance(value, int) else pl.multiple_of(value, size)


def backward_kernel(block, past, n_blocks, head, n_pieces, n_parts, *refs):
    offsets_ref, windows_ref, *refs = refs
    pieces, refs = refs[:n_pieces], refs[n_pieces:]
    key_parts, refs = refs[:n_parts], refs[n_parts:]
    value_parts, refs = refs[:n_parts], refs[n_parts:]
    dq_ref, *refs = refs
    sums, refs = refs[:n_parts], refs[n_parts:]
    held_ref, k_ref, v_ref, kt_ref, bias_ref, p_ref, gp_ref, dk_acc, dv_acc, sems = refs

    depth_id, seq_id = lax.axis_index("depth"), lax.axis_index("seq")
    shift = offsets_ref[depth_id]
    span = windows_ref[depth_id]
    seq_total = n_blocks * block
    part_rows = seq_total // n_parts
    tok_rows = held_ref.shape[2]

    def part_at(n):
        return pl.ds(pl.multiple_of((depth_id ^ n) * part_rows, part_rows) if n_parts > 1 else 0, part_rows)

    columns = pl.ds(head * HEAD_DIM, HEAD_DIM)
    copies = [(part.at[:, columns], k_ref.at[part_at(n)]) for n, part in enumerate(key_parts)]
    copies += [(part.at[:, columns], v_ref.at[part_at(n)]) for n, part in enumerate(value_parts)]
    for k in range(n_pieces):
        copies.append((pieces[k], held_ref.at[seq_id ^ k] if n_pieces > 1 else held_ref))
    copies = [
        pltpu.make_async_copy(source, target, sems.at[n]) for n, (source, target) in enumerate(copies)
    ]
    for copy in copies:
        copy.start()
    dk_acc[...] = jnp.zeros_like(dk_acc)
    dv_acc[...] = jnp.zeros_like(dv_acc)
    ahead = lax.broadcasted_iota(jnp.int32, (8, block), 0) - lax.broadcasted_iota(
        jnp.int32, (8, block), 1
    )
    for back in range(past + 1):
        for row in range(0, block, 8):
            lead = row - back * block
            keep = ahead > shift - span - lead
            if lead + 7 > 0:
                keep = keep & (ahead <= shift - lead)
            bias_ref[back, pl.ds(row, 8), :] = jnp.where(keep, 0.0, -jnp.inf)
    for copy in copies[:n_parts]:
        copy.wait()
    kt_ref[...] = k_ref[...].T
    for copy in copies[n_parts:]:
        copy.wait()

    def step(number, n_past):
        first_row = aligned(number * block, block)
        per_block = block // tok_rows
        held = pl.ds(number * per_block, per_block)
        query = held_ref[held, 0].reshape(block, HEAD_DIM)
        grad = held_ref[held, 1].reshape(block, HEAD_DIM)
        edge_first = aligned(jnp.minimum(first_row + block, seq_total - EDGE), EDGE)
        edge_key = edge_first + lax.broadcasted_iota(jnp.int32, (EDGE, block), 0)
        edge_query = first_row + lax.broadcasted_iota(jnp.int32, (EDGE, block), 1)
        edge_in = (edge_key >= first_row + block) & (edge_key - edge_query <= shift)
        tiles = [
            (aligned((number - back) * block, block), block, back * block, back)
            for back in range(n_past + 1)
        ]
        tiles.append((edge_first, EDGE, (past + 1) * block, None))

        highest = jnp.full((1, block), LOWEST, jnp.float32)
        total = jnp.zeros((1, block), jnp.float32)
        dotted = jnp.zeros((1, block), jnp.float32)
        highs = []
        for key_first, rows, at, back in tiles:
            score = nt_dot(k_ref[pl.ds(key_first, rows), :], query)
            if back is None:
                score = jnp.where(edge_in, score, -jnp.inf)
            else:
                score = score + bias_ref[back]
            now = jnp.maximum(highest, jnp.max(score, axis=0, keepdims=True))
            part = jnp.exp2((score - now) * EXP2_SCALE)
            grad_prob = nt_dot(v_ref[pl.ds(key_first, rows), :], grad)
            p_ref[pl.ds(at, rows), :] = part
            gp_ref[pl.ds(at, rows), :] = grad_prob
            less = jnp.exp2((highest - now) * EXP2_SCALE)
            total = total * less + jnp.sum(part, axis=0, keepdims=True)
            dotted = dotted * less + jnp.sum(part * grad_prob, axis=0, keepdims=True)
            highest = now
            highs.append(now)
        inverse = 1.0 / total
        row_dot = dotted * inverse

        dq_t = jnp.zeros((HEAD_DIM, block), jnp.float32)
        for (key_first, rows, at, back), high in zip(tiles, highs, strict=True):
            prob = p_ref[pl.ds(at, rows), :] * (inverse * jnp.exp2((high - highest) * EXP2_SCALE))
            weight = prob.astype(jnp.bfloat16)
            grad_score = (prob * (gp_ref[pl.ds(at, rows), :] - row_dot)).astype(jnp.bfloat16)
            here = pl.ds(key_first, rows)
            dv_acc[here, :] += nn_dot(weight, grad)
            dk_acc[here, :] += nn_dot(grad_score, query)
            if back is None:
                dq_t = dq_t + lax.dot_general(
                    k_ref[here, :], grad_score, (((0,), (0,)), ((), ())),
                    preferred_element_type=jnp.float32,
                )
            else:
                dq_t = dq_t + nn_dot(kt_ref[:, here], grad_score)
        dq_ref[held] = (
            (dq_t * SCALING).T.astype(jnp.bfloat16).reshape(per_block, tok_rows, HEAD_DIM)
        )

    for number in range(past):
        step(number, number)

    @pl.loop(past, n_blocks)
    def _(number):
        step(number, past)

    for n in range(n_parts):
        sums[n][0] = (dk_acc[part_at(n), :] * SCALING).astype(jnp.bfloat16)
        sums[n][1] = dv_acc[part_at(n), :].astype(jnp.bfloat16)


def attention_backward(offsets, windows, pieces, key_parts, value_parts, head):
    n_pieces, n_parts = len(pieces), len(key_parts)
    tok_rows = pieces[0].shape[-2]
    seq_total = key_parts[0].shape[0] * n_parts
    sources = seq_total // tok_rows
    block = min(2 * tok_rows, seq_total)
    n_blocks = seq_total // block
    past = min(-(-WIN // block), n_blocks - 1)
    rows = (past + 1) * block + EDGE
    pairs = seq_total * rows
    f32, bf16 = jnp.float32, jnp.bfloat16
    sums_shape = (2, seq_total // n_parts, HEAD_DIM)
    dq, *sums = pl.pallas_call(
        functools.partial(backward_kernel, block, past, n_blocks, head, n_pieces, n_parts),
        in_specs=[pl.BlockSpec(memory_space=pltpu.SMEM)] * 2
        + [pl.BlockSpec(memory_space=pl.ANY)] * (n_pieces + 2 * n_parts),
        out_specs=[pl.BlockSpec(memory_space=pltpu.VMEM)] * (1 + n_parts),
        scratch_shapes=[
            pltpu.VMEM((sources, 2, tok_rows, HEAD_DIM), bf16),
            pltpu.VMEM((seq_total, HEAD_DIM), bf16),
            pltpu.VMEM((seq_total, HEAD_DIM), bf16),
            pltpu.VMEM((HEAD_DIM, seq_total), bf16),
            pltpu.VMEM((past + 1, block, block), f32),
            pltpu.VMEM((rows, block), f32),
            pltpu.VMEM((rows, block), f32),
            pltpu.VMEM((seq_total, HEAD_DIM), f32),
            pltpu.VMEM((seq_total, HEAD_DIM), f32),
            pltpu.SemaphoreType.DMA((n_pieces + 2 * n_parts,)),
        ],
        out_shape=[jax.ShapeDtypeStruct((sources, tok_rows, HEAD_DIM), bf16)]
        + [jax.ShapeDtypeStruct(sums_shape, bf16)] * n_parts,
        cost_estimate=pl.CostEstimate(
            flops=10 * pairs * HEAD_DIM, bytes_accessed=14 * seq_total * HEAD_DIM, transcendentals=pairs
        ),
    )(offsets, windows, *pieces, *key_parts, *value_parts)
    return dq, sums


def pack(head, heads, queries, grad_out, n_outs):
    tok_rows, model_width = queries.shape
    parts = model_width // (heads * HEAD_DIM)
    shape = (2, tok_rows, HEAD_DIM)

    def kernel(q_ref, g_ref, *refs):
        outs, (held, in_sems, out_sems) = refs[:n_outs], refs[n_outs:]
        seq_id = lax.axis_index("seq")
        loads, stores = [], []
        for k in range(parts):
            dest = seq_id ^ k if n_outs > 1 else k
            start = pl.multiple_of((dest * heads + head) * HEAD_DIM, HEAD_DIM)
            for a, ref in enumerate((q_ref, g_ref)):
                loads.append(
                    pltpu.make_async_copy(
                        ref.at[:, pl.ds(start, HEAD_DIM)], held.at[k, a], in_sems.at[k, a]
                    )
                )
            target = outs[k] if n_outs > 1 else outs[0].at[k]
            stores.append(pltpu.make_async_copy(held.at[k], target, out_sems.at[k]))
        for load in loads:
            load.start()
        for k in range(parts):
            loads[2 * k].wait()
            loads[2 * k + 1].wait()
            stores[k].start()
        for store in stores:
            store.wait()

    return pl.pallas_call(
        kernel,
        in_specs=[pl.BlockSpec(memory_space=pl.ANY)] * 2,
        out_specs=[pl.BlockSpec(memory_space=pl.ANY)] * n_outs,
        out_shape=[jax.ShapeDtypeStruct(shape if n_outs > 1 else (parts, *shape), jnp.bfloat16)] * n_outs,
        scratch_shapes=[
            pltpu.VMEM((parts, *shape), jnp.bfloat16),
            pltpu.SemaphoreType.DMA((parts, 2)),
            pltpu.SemaphoreType.DMA((parts,)),
        ],
        cost_estimate=pl.CostEstimate(
            flops=0, bytes_accessed=4 * parts * math.prod(shape), transcendentals=0
        ),
    )(queries, grad_out)


def unpack(back, tok_rows, model_width):
    heads = len(back)
    parts = back[0].shape[0]

    def kernel(*refs):
        ins, out, sems = refs[:heads], refs[heads], refs[heads + 1]
        copies = []
        for head in range(heads):
            for d in range(parts):
                columns = pl.ds((d * heads + head) * HEAD_DIM, HEAD_DIM)
                copies.append(
                    pltpu.make_async_copy(ins[head].at[d], out.at[:, columns], sems.at[head, d])
                )
        for copy in copies:
            copy.start()
        for copy in copies:
            copy.wait()

    return pl.pallas_call(
        kernel,
        in_specs=[pl.BlockSpec(memory_space=pl.ANY)] * heads,
        out_specs=pl.BlockSpec(memory_space=pltpu.VMEM),
        out_shape=jax.ShapeDtypeStruct((tok_rows, model_width), jnp.bfloat16),
        scratch_shapes=[pltpu.SemaphoreType.DMA((heads, parts))],
        compiler_params=pltpu.CompilerParams(vmem_limit_bytes=8 * 2**20),
        name="unpack",
    )(*back)


def on_device(queries, grad_out, key_states, value_states, offsets, windows):
    depths = lax.axis_size("depth")
    parts = lax.axis_size("seq")
    tok_rows, model_width = queries.shape[1:]
    heads = key_states.shape[1] // HEAD_DIM
    queries = queries.reshape(tok_rows, model_width)
    grad_out = grad_out.reshape(tok_rows, model_width)

    def received(head):
        if head > 0 and parts & (parts - 1) == 0:
            sent = pack(head, heads, queries, grad_out, parts)
            landed = [sent[0]]
            for k in range(1, parts):
                landed.append(lax.ppermute(sent[k], "seq", [(i, i ^ k) for i in range(parts)]))
            return landed
        (sent,) = pack(head, heads, queries, grad_out, 1)
        return [lax.all_to_all(sent, "seq", split_axis=0, concat_axis=0, tiled=True)]

    pieces = [received(head) for head in range(heads)]

    swap = [(0, 1), (1, 0)]
    if depths == 2:
        key_parts = [key_states, lax.ppermute(key_states, "depth", swap)]
        value_parts = [value_states, lax.ppermute(value_states, "depth", swap)]
    else:
        key_parts = [lax.all_gather(key_states, "depth", axis=0, tiled=True)]
        value_parts = [lax.all_gather(value_states, "depth", axis=0, tiled=True)]

    def over_depths(sums):
        if depths == 2:
            other = lax.ppermute(sums[1], "depth", swap)
            return (sums[0].astype(jnp.float32) + other.astype(jnp.float32)).astype(jnp.bfloat16)
        return lax.psum_scatter(sums[0], "depth", scatter_dimension=1, tiled=True)

    back, totals = [], []
    for head in range(heads):
        dq, sums = attention_backward(offsets, windows, pieces[head], key_parts, value_parts, head)
        back.append(lax.all_to_all(dq, "seq", split_axis=0, concat_axis=0, tiled=True))
        totals.append(over_depths(sums))

    return (
        unpack(back, tok_rows, model_width).reshape(1, tok_rows, model_width),
        jnp.concatenate([total[0] for total in totals], axis=1),
        jnp.concatenate([total[1] for total in totals], axis=1),
    )


def solution(mesh):
    in_specs = (
        P("depth", "seq", None),
        P("depth", "seq", None),
        P("depth", "seq"),
        P("depth", "seq"),
        P(),
        P(),
    )
    out_specs = (P("depth", "seq", None), P("depth", "seq"), P("depth", "seq"))
    return jax.shard_map(
        on_device, mesh=mesh, in_specs=in_specs, out_specs=out_specs, check_vma=False
    )
```

```python
import functools
import math

import jax
import jax.numpy as jnp
from jax import lax
from jax.experimental import pallas as pl
from jax.experimental.pallas import tpu as pltpu
from jax.sharding import PartitionSpec as P


HEAD_DIM = 128
WIN = 1024
EDGE = 16
SCALING = 1.0 / math.sqrt(HEAD_DIM)
EXP2_SCALE = SCALING * math.log2(math.e)
LOWEST = -1e30


def nt_dot(a, b):
    return lax.dot_general(a, b, (((1,), (1,)), ((), ())), preferred_element_type=jnp.float32)


def nn_dot(a, b):
    return lax.dot_general(a, b, (((1,), (0,)), ((), ())), preferred_element_type=jnp.float32)


def aligned(value, size):
    return value if isinstance(value, int) else pl.multiple_of(value, size)


def backward_kernel(block, past, n_blocks, head, n_pieces, n_parts, *refs):
    offsets_ref, windows_ref, *refs = refs
    pieces, refs = refs[:n_pieces], refs[n_pieces:]
    key_parts, refs = refs[:n_parts], refs[n_parts:]
    value_parts, refs = refs[:n_parts], refs[n_parts:]
    dq_ref, *refs = refs
    sums, refs = refs[:n_parts], refs[n_parts:]
    held_ref, k_ref, v_ref, kt_ref, bias_ref, p_refs, gp_refs, dk_acc, dv_acc, sems = refs

    depth_id, seq_id = lax.axis_index("depth"), lax.axis_index("seq")
    shift = offsets_ref[depth_id]
    span = windows_ref[depth_id]
    seq_total = n_blocks * block
    part_rows = seq_total // n_parts
    tok_rows = held_ref.shape[2]

    def part_at(n):
        return pl.ds(pl.multiple_of((depth_id ^ n) * part_rows, part_rows) if n_parts > 1 else 0, part_rows)

    columns = pl.ds(head * HEAD_DIM, HEAD_DIM)
    copies = [(part.at[:, columns], k_ref.at[part_at(n)]) for n, part in enumerate(key_parts)]
    copies += [(part.at[:, columns], v_ref.at[part_at(n)]) for n, part in enumerate(value_parts)]
    for k in range(n_pieces):
        copies.append((pieces[k], held_ref.at[seq_id ^ k] if n_pieces > 1 else held_ref))
    copies = [
        pltpu.make_async_copy(source, target, sems.at[n]) for n, (source, target) in enumerate(copies)
    ]
    for copy in copies:
        copy.start()
    dk_acc[...] = jnp.zeros_like(dk_acc)
    dv_acc[...] = jnp.zeros_like(dv_acc)
    ahead = lax.broadcasted_iota(jnp.int32, (8, block), 0) - lax.broadcasted_iota(
        jnp.int32, (8, block), 1
    )
    for back in range(past + 1):
        for row in range(0, block, 8):
            lead = row - back * block
            keep = ahead > shift - span - lead
            if lead + 7 > 0:
                keep = keep & (ahead <= shift - lead)
            bias_ref[back, pl.ds(row, 8), :] = jnp.where(keep, 0.0, -jnp.inf)
    for copy in copies[:n_parts]:
        copy.wait()
    kt_ref[...] = k_ref[...].T
    for copy in copies[n_parts:]:
        copy.wait()

    def step(number, n_past, odd):
        p_ref, gp_ref = p_refs[odd], gp_refs[odd]
        first_row = aligned(number * block, block)
        per_block = block // tok_rows
        held = pl.ds(number * per_block, per_block)
        query = held_ref[held, 0].reshape(block, HEAD_DIM)
        grad = held_ref[held, 1].reshape(block, HEAD_DIM)
        edge_first = aligned(jnp.minimum(first_row + block, seq_total - EDGE), EDGE)
        edge_key = edge_first + lax.broadcasted_iota(jnp.int32, (EDGE, block), 0)
        edge_query = first_row + lax.broadcasted_iota(jnp.int32, (EDGE, block), 1)
        edge_in = (edge_key >= first_row + block) & (edge_key - edge_query <= shift)
        tiles = [
            (aligned((number - back) * block, block), block, back * block, back)
            for back in range(n_past + 1)
        ]
        tiles.append((edge_first, EDGE, (past + 1) * block, None))

        highest = jnp.full((1, block), LOWEST, jnp.float32)
        total = jnp.zeros((1, block), jnp.float32)
        dotted = jnp.zeros((1, block), jnp.float32)
        highs = []
        for key_first, rows, at, back in tiles:
            score = nt_dot(k_ref[pl.ds(key_first, rows), :], query)
            if back is None:
                score = jnp.where(edge_in, score, -jnp.inf)
            else:
                score = score + bias_ref[back]
            now = jnp.maximum(highest, jnp.max(score, axis=0, keepdims=True))
            part = jnp.exp2((score - now) * EXP2_SCALE)
            grad_prob = nt_dot(v_ref[pl.ds(key_first, rows), :], grad)
            p_ref[pl.ds(at, rows), :] = part
            gp_ref[pl.ds(at, rows), :] = grad_prob
            less = jnp.exp2((highest - now) * EXP2_SCALE)
            total = total * less + jnp.sum(part, axis=0, keepdims=True)
            dotted = dotted * less + jnp.sum(part * grad_prob, axis=0, keepdims=True)
            highest = now
            highs.append(now)
        inverse = 1.0 / total
        row_dot = dotted * inverse

        dq_t = jnp.zeros((HEAD_DIM, block), jnp.float32)
        for (key_first, rows, at, back), high in zip(tiles, highs, strict=True):
            prob = p_ref[pl.ds(at, rows), :] * (inverse * jnp.exp2((high - highest) * EXP2_SCALE))
            weight = prob.astype(jnp.bfloat16)
            grad_score = (prob * (gp_ref[pl.ds(at, rows), :] - row_dot)).astype(jnp.bfloat16)
            here = pl.ds(key_first, rows)
            dv_acc[here, :] += nn_dot(weight, grad)
            dk_acc[here, :] += nn_dot(grad_score, query)
            if back is None:
                dq_t = dq_t + lax.dot_general(
                    k_ref[here, :], grad_score, (((0,), (0,)), ((), ())),
                    preferred_element_type=jnp.float32,
                )
            else:
                dq_t = dq_t + nn_dot(kt_ref[:, here], grad_score)
        dq_ref[held] = (
            (dq_t * SCALING).T.astype(jnp.bfloat16).reshape(per_block, tok_rows, HEAD_DIM)
        )

    for number in range(past):
        step(number, number, number % 2)

    @pl.loop(0, (n_blocks - past) // 2)
    def _(pair):
        for n in range(2):
            step(past + 2 * pair + n, past, n)

    if (n_blocks - past) % 2:
        step(n_blocks - 1, past, 0)

    for n in range(n_parts):
        sums[n][0] = (dk_acc[part_at(n), :] * SCALING).astype(jnp.bfloat16)
        sums[n][1] = dv_acc[part_at(n), :].astype(jnp.bfloat16)


def attention_backward(offsets, windows, pieces, key_parts, value_parts, head):
    n_pieces, n_parts = len(pieces), len(key_parts)
    tok_rows = pieces[0].shape[-2]
    seq_total = key_parts[0].shape[0] * n_parts
    sources = seq_total // tok_rows
    block = min(2 * tok_rows, seq_total)
    n_blocks = seq_total // block
    past = min(-(-WIN // block), n_blocks - 1)
    rows = (past + 1) * block + EDGE
    pairs = seq_total * rows
    f32, bf16 = jnp.float32, jnp.bfloat16
    sums_shape = (2, seq_total // n_parts, HEAD_DIM)
    dq, *sums = pl.pallas_call(
        functools.partial(backward_kernel, block, past, n_blocks, head, n_pieces, n_parts),
        in_specs=[pl.BlockSpec(memory_space=pltpu.SMEM)] * 2
        + [pl.BlockSpec(memory_space=pl.ANY)] * (n_pieces + 2 * n_parts),
        out_specs=[pl.BlockSpec(memory_space=pltpu.VMEM)] * (1 + n_parts),
        scratch_shapes=[
            pltpu.VMEM((sources, 2, tok_rows, HEAD_DIM), bf16),
            pltpu.VMEM((seq_total, HEAD_DIM), bf16),
            pltpu.VMEM((seq_total, HEAD_DIM), bf16),
            pltpu.VMEM((HEAD_DIM, seq_total), bf16),
            pltpu.VMEM((past + 1, block, block), f32),
            [pltpu.VMEM((rows, block), f32)] * 2,
            [pltpu.VMEM((rows, block), f32)] * 2,
            pltpu.VMEM((seq_total, HEAD_DIM), f32),
            pltpu.VMEM((seq_total, HEAD_DIM), f32),
            pltpu.SemaphoreType.DMA((n_pieces + 2 * n_parts,)),
        ],
        out_shape=[jax.ShapeDtypeStruct((sources, tok_rows, HEAD_DIM), bf16)]
        + [jax.ShapeDtypeStruct(sums_shape, bf16)] * n_parts,
        cost_estimate=pl.CostEstimate(
            flops=10 * pairs * HEAD_DIM, bytes_accessed=14 * seq_total * HEAD_DIM, transcendentals=pairs
        ),
    )(offsets, windows, *pieces, *key_parts, *value_parts)
    return dq, sums


def pack(head, heads, queries, grad_out, n_outs):
    tok_rows, model_width = queries.shape
    parts = model_width // (heads * HEAD_DIM)
    shape = (2, tok_rows, HEAD_DIM)

    def kernel(q_ref, g_ref, *refs):
        outs, (held, in_sems, out_sems) = refs[:n_outs], refs[n_outs:]
        seq_id = lax.axis_index("seq")
        loads, stores = [], []
        for k in range(parts):
            dest = seq_id ^ k if n_outs > 1 else k
            start = pl.multiple_of((dest * heads + head) * HEAD_DIM, HEAD_DIM)
            for a, ref in enumerate((q_ref, g_ref)):
                loads.append(
                    pltpu.make_async_copy(
                        ref.at[:, pl.ds(start, HEAD_DIM)], held.at[k, a], in_sems.at[k, a]
                    )
                )
            target = outs[k] if n_outs > 1 else outs[0].at[k]
            stores.append(pltpu.make_async_copy(held.at[k], target, out_sems.at[k]))
        for load in loads:
            load.start()
        for k in range(parts):
            loads[2 * k].wait()
            loads[2 * k + 1].wait()
            stores[k].start()
        for store in stores:
            store.wait()

    return pl.pallas_call(
        kernel,
        in_specs=[pl.BlockSpec(memory_space=pl.ANY)] * 2,
        out_specs=[pl.BlockSpec(memory_space=pl.ANY)] * n_outs,
        out_shape=[jax.ShapeDtypeStruct(shape if n_outs > 1 else (parts, *shape), jnp.bfloat16)] * n_outs,
        scratch_shapes=[
            pltpu.VMEM((parts, *shape), jnp.bfloat16),
            pltpu.SemaphoreType.DMA((parts, 2)),
            pltpu.SemaphoreType.DMA((parts,)),
        ],
        cost_estimate=pl.CostEstimate(
            flops=0, bytes_accessed=4 * parts * math.prod(shape), transcendentals=0
        ),
    )(queries, grad_out)


def unpack(back, tok_rows, model_width):
    heads = len(back)
    parts = back[0].shape[0]

    def kernel(*refs):
        ins, out, sems = refs[:heads], refs[heads], refs[heads + 1]
        copies = []
        for head in range(heads):
            for d in range(parts):
                columns = pl.ds((d * heads + head) * HEAD_DIM, HEAD_DIM)
                copies.append(
                    pltpu.make_async_copy(ins[head].at[d], out.at[:, columns], sems.at[head, d])
                )
        for copy in copies:
            copy.start()
        for copy in copies:
            copy.wait()

    return pl.pallas_call(
        kernel,
        in_specs=[pl.BlockSpec(memory_space=pl.ANY)] * heads,
        out_specs=pl.BlockSpec(memory_space=pltpu.VMEM),
        out_shape=jax.ShapeDtypeStruct((tok_rows, model_width), jnp.bfloat16),
        scratch_shapes=[pltpu.SemaphoreType.DMA((heads, parts))],
        compiler_params=pltpu.CompilerParams(vmem_limit_bytes=8 * 2**20),
        name="unpack",
    )(*back)


def on_device(queries, grad_out, key_states, value_states, offsets, windows):
    depths = lax.axis_size("depth")
    parts = lax.axis_size("seq")
    tok_rows, model_width = queries.shape[1:]
    heads = key_states.shape[1] // HEAD_DIM
    queries = queries.reshape(tok_rows, model_width)
    grad_out = grad_out.reshape(tok_rows, model_width)

    def received(head):
        if head > 0 and parts & (parts - 1) == 0:
            sent = pack(head, heads, queries, grad_out, parts)
            landed = [sent[0]]
            for k in range(1, parts):
                landed.append(lax.ppermute(sent[k], "seq", [(i, i ^ k) for i in range(parts)]))
            return landed
        (sent,) = pack(head, heads, queries, grad_out, 1)
        return [lax.all_to_all(sent, "seq", split_axis=0, concat_axis=0, tiled=True)]

    pieces = [received(head) for head in range(heads)]

    swap = [(0, 1), (1, 0)]
    if depths == 2:
        key_parts = [key_states, lax.ppermute(key_states, "depth", swap)]
        value_parts = [value_states, lax.ppermute(value_states, "depth", swap)]
    else:
        key_parts = [lax.all_gather(key_states, "depth", axis=0, tiled=True)]
        value_parts = [lax.all_gather(value_states, "depth", axis=0, tiled=True)]

    def over_depths(sums):
        if depths == 2:
            other = lax.ppermute(sums[1], "depth", swap)
            return (sums[0].astype(jnp.float32) + other.astype(jnp.float32)).astype(jnp.bfloat16)
        return lax.psum_scatter(sums[0], "depth", scatter_dimension=1, tiled=True)

    back, totals = [], []
    for head in range(heads):
        dq, sums = attention_backward(offsets, windows, pieces[head], key_parts, value_parts, head)
        back.append(lax.all_to_all(dq, "seq", split_axis=0, concat_axis=0, tiled=True))
        totals.append(over_depths(sums))

    return (
        unpack(back, tok_rows, model_width).reshape(1, tok_rows, model_width),
        jnp.concatenate([total[0] for total in totals], axis=1),
        jnp.concatenate([total[1] for total in totals], axis=1),
    )


def solution(mesh):
    in_specs = (
        P("depth", "seq", None),
        P("depth", "seq", None),
        P("depth", "seq"),
        P("depth", "seq"),
        P(),
        P(),
    )
    out_specs = (P("depth", "seq", None), P("depth", "seq"), P("depth", "seq"))
    return jax.shard_map(
        on_device, mesh=mesh, in_specs=in_specs, out_specs=out_specs, check_vma=False
    )
```

```python
import functools
import math

import jax
import jax.numpy as jnp
from jax import lax
from jax.experimental import pallas as pl
from jax.experimental.pallas import tpu as pltpu
from jax.sharding import PartitionSpec as P


HEAD_DIM = 128
WIN = 1024
EDGE = 16
SCALING = 1.0 / math.sqrt(HEAD_DIM)
EXP2_SCALE = SCALING * math.log2(math.e)
LOWEST = -1e30


def nt_dot(a, b):
    return lax.dot_general(a, b, (((1,), (1,)), ((), ())), preferred_element_type=jnp.float32)


def nn_dot(a, b):
    return lax.dot_general(a, b, (((1,), (0,)), ((), ())), preferred_element_type=jnp.float32)


def aligned(value, size):
    return value if isinstance(value, int) else pl.multiple_of(value, size)


def backward_kernel(block, past, n_blocks, head, n_pieces, n_parts, *refs):
    offsets_ref, windows_ref, *refs = refs
    pieces, refs = refs[:n_pieces], refs[n_pieces:]
    key_parts, refs = refs[:n_parts], refs[n_parts:]
    value_parts, refs = refs[:n_parts], refs[n_parts:]
    dq_ref, *refs = refs
    sums, refs = refs[:n_parts], refs[n_parts:]
    held_ref, k_ref, v_ref, kt_ref, bias_ref, p_refs, gp_refs, dk_acc, dv_acc, sems = refs

    depth_id, seq_id = lax.axis_index("depth"), lax.axis_index("seq")
    shift = offsets_ref[depth_id]
    span = windows_ref[depth_id]
    seq_total = n_blocks * block
    part_rows = seq_total // n_parts
    tok_rows = held_ref.shape[2]

    def part_at(n):
        return pl.ds(pl.multiple_of((depth_id ^ n) * part_rows, part_rows) if n_parts > 1 else 0, part_rows)

    columns = pl.ds(head * HEAD_DIM, HEAD_DIM)
    copies = [(part.at[:, columns], k_ref.at[part_at(n)]) for n, part in enumerate(key_parts)]
    copies += [(part.at[:, columns], v_ref.at[part_at(n)]) for n, part in enumerate(value_parts)]
    for k in range(n_pieces):
        copies.append((pieces[k], held_ref.at[seq_id ^ k] if n_pieces > 1 else held_ref))
    copies = [
        pltpu.make_async_copy(source, target, sems.at[n]) for n, (source, target) in enumerate(copies)
    ]
    for copy in copies:
        copy.start()
    dk_acc[...] = jnp.zeros_like(dk_acc)
    dv_acc[...] = jnp.zeros_like(dv_acc)
    ahead = lax.broadcasted_iota(jnp.int32, (8, block), 0) - lax.broadcasted_iota(
        jnp.int32, (8, block), 1
    )
    for back in range(past + 1):
        for row in range(0, block, 8):
            lead = row - back * block
            keep = ahead > shift - span - lead
            if lead + 7 > 0:
                keep = keep & (ahead <= shift - lead)
            bias_ref[back, pl.ds(row, 8), :] = jnp.where(keep, 0.0, -jnp.inf)
    for copy in copies[:n_parts]:
        copy.wait()
    kt_ref[...] = k_ref[...].T
    for copy in copies[n_parts:]:
        copy.wait()

    def step(number, n_past, odd):
        p_ref, gp_ref = p_refs[odd], gp_refs[odd]
        first_row = aligned(number * block, block)
        per_block = block // tok_rows
        held = pl.ds(number * per_block, per_block)
        query = held_ref[held, 0].reshape(block, HEAD_DIM)
        grad = held_ref[held, 1].reshape(block, HEAD_DIM)
        edge_first = aligned(jnp.minimum(first_row + block, seq_total - EDGE), EDGE)
        edge_key = edge_first + lax.broadcasted_iota(jnp.int32, (EDGE, block), 0)
        edge_query = first_row + lax.broadcasted_iota(jnp.int32, (EDGE, block), 1)
        edge_in = (edge_key >= first_row + block) & (edge_key - edge_query <= shift)
        tiles = [
            (aligned((number - back) * block, block), block, back * block, back)
            for back in range(n_past + 1)
        ]
        tiles.append((edge_first, EDGE, (past + 1) * block, None))

        highest = jnp.full((1, block), LOWEST, jnp.float32)
        total = jnp.zeros((1, block), jnp.float32)
        dotted = jnp.zeros((1, block), jnp.float32)
        highs = []
        for key_first, rows, at, back in tiles:
            score = nt_dot(k_ref[pl.ds(key_first, rows), :], query)
            if back is None:
                score = jnp.where(edge_in, score, -jnp.inf)
            else:
                score = score + bias_ref[back]
            now = jnp.maximum(highest, jnp.max(score, axis=0, keepdims=True))
            part = jnp.exp2((score - now) * EXP2_SCALE)
            grad_prob = nt_dot(v_ref[pl.ds(key_first, rows), :], grad)
            p_ref[pl.ds(at, rows), :] = part
            gp_ref[pl.ds(at, rows), :] = grad_prob
            less = jnp.exp2((highest - now) * EXP2_SCALE)
            total = total * less + jnp.sum(part, axis=0, keepdims=True)
            dotted = dotted * less + jnp.sum(part * grad_prob, axis=0, keepdims=True)
            highest = now
            highs.append(now)
        inverse = 1.0 / total
        row_dot = dotted * inverse

        dq_t = jnp.zeros((HEAD_DIM, block), jnp.float32)
        for (key_first, rows, at, back), high in zip(tiles, highs, strict=True):
            prob = p_ref[pl.ds(at, rows), :] * (inverse * jnp.exp2((high - highest) * EXP2_SCALE))
            weight = prob.astype(jnp.bfloat16)
            grad_score = (prob * (gp_ref[pl.ds(at, rows), :] - row_dot)).astype(jnp.bfloat16)
            here = pl.ds(key_first, rows)
            dv_acc[here, :] += nn_dot(weight, grad)
            dk_acc[here, :] += nn_dot(grad_score, query)
            if back is None:
                dq_t = dq_t + lax.dot_general(
                    k_ref[here, :], grad_score, (((0,), (0,)), ((), ())),
                    preferred_element_type=jnp.float32,
                )
            else:
                dq_t = dq_t + nn_dot(kt_ref[:, here], grad_score)
        dq_ref[held] = (
            (dq_t * SCALING).T.astype(jnp.bfloat16).reshape(per_block, tok_rows, HEAD_DIM)
        )

    for number in range(past):
        step(number, number, number % 2)

    @pl.loop(0, (n_blocks - past) // 2)
    def _(pair):
        for n in range(2):
            step(past + 2 * pair + n, past, n)

    if (n_blocks - past) % 2:
        step(n_blocks - 1, past, 0)

    for n in range(n_parts):
        sums[n][0] = (dk_acc[part_at(n), :] * SCALING).astype(jnp.bfloat16)
        sums[n][1] = dv_acc[part_at(n), :].astype(jnp.bfloat16)


def attention_backward(offsets, windows, pieces, key_parts, value_parts, head):
    n_pieces, n_parts = len(pieces), len(key_parts)
    tok_rows = pieces[0].shape[-2]
    seq_total = key_parts[0].shape[0] * n_parts
    sources = seq_total // tok_rows
    block = min(2 * tok_rows, seq_total)
    n_blocks = seq_total // block
    past = min(-(-WIN // block), n_blocks - 1)
    rows = (past + 1) * block + EDGE
    pairs = seq_total * rows
    f32, bf16 = jnp.float32, jnp.bfloat16
    sums_shape = (2, seq_total // n_parts, HEAD_DIM)
    dq, *sums = pl.pallas_call(
        functools.partial(backward_kernel, block, past, n_blocks, head, n_pieces, n_parts),
        in_specs=[pl.BlockSpec(memory_space=pltpu.SMEM)] * 2
        + [pl.BlockSpec(memory_space=pl.ANY)] * (n_pieces + 2 * n_parts),
        out_specs=[pl.BlockSpec(memory_space=pltpu.VMEM)] * (1 + n_parts),
        scratch_shapes=[
            pltpu.VMEM((sources, 2, tok_rows, HEAD_DIM), bf16),
            pltpu.VMEM((seq_total, HEAD_DIM), bf16),
            pltpu.VMEM((seq_total, HEAD_DIM), bf16),
            pltpu.VMEM((HEAD_DIM, seq_total), bf16),
            pltpu.VMEM((past + 1, block, block), f32),
            [pltpu.VMEM((rows, block), f32)] * 2,
            [pltpu.VMEM((rows, block), f32)] * 2,
            pltpu.VMEM((seq_total, HEAD_DIM), f32),
            pltpu.VMEM((seq_total, HEAD_DIM), f32),
            pltpu.SemaphoreType.DMA((n_pieces + 2 * n_parts,)),
        ],
        out_shape=[jax.ShapeDtypeStruct((sources, tok_rows, HEAD_DIM), bf16)]
        + [jax.ShapeDtypeStruct(sums_shape, bf16)] * n_parts,
        cost_estimate=pl.CostEstimate(
            flops=10 * pairs * HEAD_DIM, bytes_accessed=14 * seq_total * HEAD_DIM, transcendentals=pairs
        ),
    )(offsets, windows, *pieces, *key_parts, *value_parts)
    return dq, sums


def pack(head, heads, queries, grad_out, n_outs):
    tok_rows, model_width = queries.shape
    parts = model_width // (heads * HEAD_DIM)
    shape = (2, tok_rows, HEAD_DIM)

    def kernel(q_ref, g_ref, *refs):
        outs, (held, in_sems, out_sems) = refs[:n_outs], refs[n_outs:]
        seq_id = lax.axis_index("seq")
        loads, stores = [], []
        for k in range(parts):
            dest = seq_id ^ k if n_outs > 1 else k
            start = pl.multiple_of((dest * heads + head) * HEAD_DIM, HEAD_DIM)
            for a, ref in enumerate((q_ref, g_ref)):
                loads.append(
                    pltpu.make_async_copy(
                        ref.at[:, pl.ds(start, HEAD_DIM)], held.at[k, a], in_sems.at[k, a]
                    )
                )
            target = outs[k] if n_outs > 1 else outs[0].at[k]
            stores.append(pltpu.make_async_copy(held.at[k], target, out_sems.at[k]))
        for load in loads:
            load.start()
        for k in range(parts):
            loads[2 * k].wait()
            loads[2 * k + 1].wait()
            stores[k].start()
        for store in stores:
            store.wait()

    return pl.pallas_call(
        kernel,
        in_specs=[pl.BlockSpec(memory_space=pl.ANY)] * 2,
        out_specs=[pl.BlockSpec(memory_space=pl.ANY)] * n_outs,
        out_shape=[jax.ShapeDtypeStruct(shape if n_outs > 1 else (parts, *shape), jnp.bfloat16)] * n_outs,
        scratch_shapes=[
            pltpu.VMEM((parts, *shape), jnp.bfloat16),
            pltpu.SemaphoreType.DMA((parts, 2)),
            pltpu.SemaphoreType.DMA((parts,)),
        ],
        cost_estimate=pl.CostEstimate(
            flops=0, bytes_accessed=4 * parts * math.prod(shape), transcendentals=0
        ),
    )(queries, grad_out)


def unpack(arrived, head, heads, tok_rows, so_far):
    parts = arrived.shape[0]

    def kernel(*refs):
        source, out, sems = refs[0], refs[-2], refs[-1]
        copies = [
            pltpu.make_async_copy(
                source.at[d], out.at[:, pl.ds((d * heads + head) * HEAD_DIM, HEAD_DIM)], sems.at[d]
            )
            for d in range(parts)
        ]
        for copy in copies:
            copy.start()
        for copy in copies:
            copy.wait()

    args = [arrived] if so_far is None else [arrived, so_far]
    return pl.pallas_call(
        kernel,
        in_specs=[pl.BlockSpec(memory_space=pl.ANY)] * len(args),
        out_specs=pl.BlockSpec(memory_space=pl.ANY),
        out_shape=jax.ShapeDtypeStruct((tok_rows, parts * heads * HEAD_DIM), jnp.bfloat16),
        input_output_aliases={} if so_far is None else {1: 0},
        scratch_shapes=[pltpu.SemaphoreType.DMA((parts,))],
        compiler_params=pltpu.CompilerParams(vmem_limit_bytes=32 * 2**20),
    )(*args)


def on_device(queries, grad_out, key_states, value_states, offsets, windows):
    depths = lax.axis_size("depth")
    parts = lax.axis_size("seq")
    tok_rows, model_width = queries.shape[1:]
    heads = key_states.shape[1] // HEAD_DIM
    queries = queries.reshape(tok_rows, model_width)
    grad_out = grad_out.reshape(tok_rows, model_width)

    def received(head):
        if head > 0 and parts & (parts - 1) == 0:
            sent = pack(head, heads, queries, grad_out, parts)
            landed = [sent[0]]
            for k in range(1, parts):
                landed.append(lax.ppermute(sent[k], "seq", [(i, i ^ k) for i in range(parts)]))
            return landed
        (sent,) = pack(head, heads, queries, grad_out, 1)
        return [lax.all_to_all(sent, "seq", split_axis=0, concat_axis=0, tiled=True)]

    pieces = [received(head) for head in range(heads)]

    swap = [(0, 1), (1, 0)]
    if depths == 2:
        key_parts = [key_states, lax.ppermute(key_states, "depth", swap)]
        value_parts = [value_states, lax.ppermute(value_states, "depth", swap)]
    else:
        key_parts = [lax.all_gather(key_states, "depth", axis=0, tiled=True)]
        value_parts = [lax.all_gather(value_states, "depth", axis=0, tiled=True)]

    def over_depths(sums):
        if depths == 2:
            other = lax.ppermute(sums[1], "depth", swap)
            return (sums[0].astype(jnp.float32) + other.astype(jnp.float32)).astype(jnp.bfloat16)
        return lax.psum_scatter(sums[0], "depth", scatter_dimension=1, tiled=True)

    back, totals = [], []
    for head in range(heads):
        dq, sums = attention_backward(offsets, windows, pieces[head], key_parts, value_parts, head)
        back.append(lax.all_to_all(dq, "seq", split_axis=0, concat_axis=0, tiled=True))
        totals.append(over_depths(sums))

    whole = None
    for head in range(heads):
        whole = unpack(back[head], head, heads, tok_rows, whole)
    return (
        whole.reshape(1, tok_rows, model_width),
        jnp.concatenate([total[0] for total in totals], axis=1),
        jnp.concatenate([total[1] for total in totals], axis=1),
    )


def solution(mesh):
    in_specs = (
        P("depth", "seq", None),
        P("depth", "seq", None),
        P("depth", "seq"),
        P("depth", "seq"),
        P(),
        P(),
    )
    out_specs = (P("depth", "seq", None), P("depth", "seq"), P("depth", "seq"))
    return jax.shard_map(on_device, mesh=mesh, in_specs=in_specs, out_specs=out_specs, check_vma=False)
```
